256 devices in a mesh: row: 16 (over z, y_hi), col: 16 (over x, y_lo, core).
Axes of the slice: x: 4, y: 4 (y_hi: 2, y_lo: 2; y = y_hi * 2 + y_lo), z: 8, core: 2. Of those that a mesh axis runs over, the one named last changes fastest.
Arguments:
- amplitudes: float32 [16, 16, 400, 400], P('row', None, 'col'), may hold values from -6 to 6
- integrals: float32 [64, 64, 400, 400], P('row', None, 'col'), may hold values from -0.015625 to 0.015625
- rest: float32 [16, 16, 64, 64], P('col', None, 'row'), may hold values from -6 to 6
- occ_energy: float32 [16], replicated, may hold values from -2 to -0.5
- vir_energy: float32 [64], replicated, may hold values from 0.5 to 3
Outputs:
- new_amps: float32 [16, 16, 64, 64], P('col', None, 'row')
The draws below stay inside these ranges and needn't reach their ends.
All inputs are finite; a program needn't handle non-finite values.
Results may differ from the reference program's by a relative error of at most 0.000057.
Values sent between devices are 32-bit elements; how exact they have to be, the bound alone decides.
No kernel may reach another device: no remote copies, remote signals or barrier semaphores. Data moves between devices by JAX's collectives and lax.ppermute only.
A program may use at most 128 MiB of HBM per device.

```python
import jax
import jax.numpy as jnp
from jax import lax

NV = 400
NO = 16
W = 64


def block_levels(rng, shape, pieces, least, top_value):
    factor_of, own = 1.0, jax.random.fold_in(rng, 6)
    for axis_at, parts in pieces:
        steps = jnp.exp(jax.random.uniform(jax.random.fold_in(own, axis_at), (parts,), jnp.float32, least / len(pieces), top_value / len(pieces)))
        factor_of = factor_of * jnp.repeat(steps, shape[axis_at] // parts).reshape([-1 if axis == axis_at else 1 for axis in range(len(shape))])
    return factor_of


def bell_draw(stream_key, dims, deviation, bound, cuts=(), held_as=jnp.bfloat16):
    entries = deviation * jax.random.normal(stream_key, dims, jnp.float32)
    if cuts:
        entries = entries * block_levels(stream_key, dims, cuts, -0.22, 0.18)
    return jnp.clip(entries, -bound, bound).astype(held_as)


def setup_inputs(seed: int = 0) -> dict:
    seeds = jax.random.split(jax.random.key(seed), 6)
    return {
        "amplitudes": bell_draw(seeds[0], (NO, NO, NV, NV), 1.0, 6.0, ((0, 16), (2, 16)), jnp.float32),
        "integrals": bell_draw(seeds[1], (W, W, NV, NV), (NV * NV) ** -0.5, 0.015625, ((0, 16), (2, 16)), jnp.float32),
        "rest": bell_draw(seeds[2], (NO, NO, W, W), 1.0, 6.0, ((0, 16), (2, 16)), jnp.float32),
        "occ_energy": jnp.clip(jax.random.uniform(seeds[3], (NO,), jnp.float32, -2.0, -0.5), -2.0, -0.5),
        "vir_energy": jnp.clip(jax.random.uniform(seeds[4], (W,), jnp.float32, 0.5, 3.0), 0.5, 3.0),
    }


def reference(amplitudes, integrals, rest, occ_energy, vir_energy):
    flattened = amplitudes.reshape(NO * NO, NV * NV)

    def one_virtual(integral_block):
        return jnp.dot(flattened, integral_block.reshape(W, NV * NV).T, precision=lax.Precision.HIGHEST, preferred_element_type=jnp.float32)

    stacked = lax.map(one_virtual, integrals)
    ladder = jnp.transpose(stacked, (1, 0, 2)).reshape(NO, NO, W, W)
    mirror = jnp.transpose(ladder, (1, 0, 3, 2))
    denominator = vir_energy[None, None, :, None] + vir_energy[None, None, None, :] - occ_energy[:, None, None, None] - occ_energy[None, :, None, None]
    return (ladder + mirror + rest) / denominator
```

```python
import jax
import jax.numpy as jnp
from jax import lax
from jax.experimental import pallas as pl
from jax.experimental.pallas import tpu as pltpu
from jax.sharding import PartitionSpec as P


NR, NC = 16, 16
NZ = 8
ND = 400
LANES = 128
NJ, NAB = 16, 256
TA, TB = 50, 29
F32, BF16 = jnp.float32, jnp.bfloat16


def rows_of_rest(x, n):
    parts = [x(c) for c in range(n)]
    if n < 8:
        parts.append(jnp.zeros(parts[0].shape[:-1] + (LANES - 16 * n,), F32))
    return jnp.concatenate(parts, axis=-1)


def pack_t_kernel(t_ref, a_ref, b_ref):
    for ref, at, c0, n in ((a_ref, 0, 0, 8), (a_ref, 25, 8, 8), (b_ref, 0, 16, 8), (b_ref, 25, 24, 1)):
        for c in range(n):
            for s in range(3):
                ref[at + 3 * c + s] = t_ref[c0 + c, :, LANES * s : LANES * (s + 1)]
        ref[at + 3 * n] = rows_of_rest(lambda c: t_ref[c0 + c, :, 384:400], n)


def pack_t(t):
    return pl.pallas_call(
        pack_t_kernel,
        out_shape=(
            jax.ShapeDtypeStruct((TA, NJ, LANES), F32),
            jax.ShapeDtypeStruct((TB, NJ, LANES), F32),
        ),
        name="pack_t",
    )(t)


def split(x):
    hi = x.astype(BF16)
    return hi, (x - hi.astype(F32)).astype(BF16)


def pack_v_group(v_ref, h_ref, l_ref, at, n):
    for c in range(n):
        for s in range(3):
            t = at + 3 * c + s
            h_ref[t], l_ref[t] = split(v_ref[c, :, LANES * s : LANES * (s + 1)])
    t = at + 3 * n
    h_ref[t], l_ref[t] = split(rows_of_rest(lambda c: v_ref[c, :, 384:400], n))


def pack_va_kernel(v_ref, h_ref, l_ref):
    pack_v_group(v_ref, h_ref, l_ref, 0, 8)


def pack_vb_kernel(v_ref, w_ref, h_ref, l_ref):
    pack_v_group(v_ref, h_ref, l_ref, 0, 8)
    pack_v_group(w_ref, h_ref, l_ref, 25, 1)


def pack_va(v):
    out = jax.ShapeDtypeStruct((TA, NAB, LANES), BF16)
    spec = pl.BlockSpec((25, 64, LANES), lambda g, a: (g, a, 0))
    return pl.pallas_call(
        pack_va_kernel,
        grid=(2, 4),
        in_specs=[pl.BlockSpec((None, 8, 64, ND), lambda g, a: (a, g, 0, 0))],
        out_specs=(spec, spec),
        out_shape=(out, out),
        name="pack_va",
    )(v)


def pack_vb(v):
    out = jax.ShapeDtypeStruct((TB, NAB, LANES), BF16)
    spec = pl.BlockSpec((TB, 64, LANES), lambda a: (0, a, 0))
    return pl.pallas_call(
        pack_vb_kernel,
        grid=(4,),
        in_specs=[
            pl.BlockSpec((None, 8, 64, ND), lambda a: (a, 2, 0, 0)),
            pl.BlockSpec((None, 1, 64, ND), lambda a: (a, 24, 0, 0)),
        ],
        out_specs=(spec, spec),
        out_shape=(out, out),
        name="pack_vb",
    )(v, v)


def product(t_refs, vh_ref, vl_ref, first, n):
    cat = lambda ref: jnp.concatenate([ref[first + t] for t in range(n)], axis=-1)
    hi, lo = split(jnp.concatenate([cat(r) for r in t_refs], axis=0))
    vh, vl = cat(vh_ref), cat(vl_ref)
    dims = (((1,), (1,)), ((), ()))
    both = lax.dot_general(jnp.concatenate([hi, lo], axis=0), vh, dims, preferred_element_type=F32)
    m = hi.shape[0]
    return both[:m] + both[m:] + lax.dot_general(hi, vl, dims, preferred_element_type=F32)


def product_b(refs, vh, vl):
    rows = []
    for ref in refs:
        rows += [ref.at[0], ref.at[1]] if len(ref.shape) == 4 else [ref]
    total = product(rows, vh, vl, 0, 6)
    for first, n in ((6, 6), (12, 6), (18, 6), (24, 5)):
        total += product(rows, vh, vl, first, n)
    return total


STEPS_A = 5


def dot_a_kernel(*refs):
    *t_refs, vh, vl, out = refs
    value = product(t_refs, vh, vl, 0, TA // STEPS_A)

    @pl.when(pl.program_id(0) == 0)
    def _():
        out[...] = value

    @pl.when(pl.program_id(0) > 0)
    def _():
        out[...] += value


def dot_a(blocks, vh, vl):
    n = len(blocks)
    tiles = TA // STEPS_A
    tspec = pl.BlockSpec((tiles, NJ, LANES), lambda s: (s, 0, 0))
    vspec = pl.BlockSpec((tiles, NAB, LANES), lambda s: (s, 0, 0))
    return pl.pallas_call(
        dot_a_kernel,
        grid=(STEPS_A,),
        in_specs=[tspec] * n + [vspec, vspec],
        out_specs=pl.BlockSpec((NJ * n, NAB), lambda s: (0, 0)),
        out_shape=jax.ShapeDtypeStruct((NJ * n, NAB), F32),
        name="dot_a",
    )(*blocks, vh, vl)


def dot_b_kernel(*refs):
    *t_refs, vh, vl, out = refs
    out[...] = product_b(t_refs, vh, vl)


def dot_b(blocks, rows, vh, vl):
    return pl.pallas_call(
        dot_b_kernel, out_shape=jax.ShapeDtypeStruct((rows, NAB), F32), name="dot_b"
    )(*blocks, vh, vl)


def absolute_row(row, dz, dy):
    return (((row >> 1) + dz) & (NZ - 1)) * 2 + ((row & 1) ^ dy)


def last_kernel(where, n1, row_ref, *refs):
    *t_refs, vh, vl, pa1, pa2, pb, out, left, right = refs
    new = product_b(t_refs, vh, vl)
    row = row_ref[0]
    for q, (dz, dy) in enumerate(where):
        here = slice(NJ * q, NJ * (q + 1))
        there = slice(NJ * (q - n1), NJ * (q - n1 + 1))
        block = pa1[here, :] + pb[here, :] if q < n1 else pa2[there, :] + new[there, :]
        at = pl.ds(pl.multiple_of(absolute_row(row, dz, dy) * NJ, NJ), NJ)
        left[at, :] = block[:, :LANES]
        right[at, :] = block[:, LANES:]
    for k in range(NC):
        for ref, lanes in ((left, slice(0, LANES)), (right, slice(LANES, NAB))):
            out[k, :NJ, lanes] = ref[NJ * k : NJ * (k + 1), :]
            out[k, NJ:, lanes] = ref[pl.ds(k, NJ, stride=NJ), :]


def last(row, where, n1, blocks, vh, vl, pa1, pa2, pb):
    return pl.pallas_call(
        lambda *refs: last_kernel(where, n1, *refs),
        in_specs=[pl.BlockSpec(memory_space=pltpu.SMEM)]
        + [pl.BlockSpec(memory_space=pltpu.VMEM)] * (len(blocks) + 5),
        out_specs=pl.BlockSpec(memory_space=pltpu.VMEM),
        out_shape=jax.ShapeDtypeStruct((NC, 2 * NJ, NAB), F32),
        scratch_shapes=[pltpu.VMEM((NAB, LANES), F32)] * 2,
        name="last",
    )(row, *blocks, vh, vl, pa1, pa2, pb)


def permute_lanes(x, source):
    lane = lax.broadcasted_iota(jnp.int32, (NAB, NAB), 1)
    one_hot = (lax.broadcasted_iota(jnp.int32, (NAB, NAB), 0) == source(lane)).astype(BF16)
    p1, r1 = x.astype(BF16), x - x.astype(BF16).astype(F32)
    p2 = r1.astype(BF16)
    p3 = (r1 - p2.astype(F32)).astype(BF16)
    y = jnp.dot(jnp.concatenate([p1, p2, p3], axis=0), one_hot, preferred_element_type=F32)
    m = x.shape[0]
    return y[:m] + y[m : 2 * m] + y[2 * m :]


def fold_kernel(r_ref, d_ref, e_ref):
    total = r_ref[0]
    for k in range(1, NC):
        total += r_ref[k]
    d_ref[...] = total[:NJ]
    mixed = permute_lanes(total[NJ:], lambda n: ((n >> 2) & 3) * 64 + (n >> 4) * 4 + (n & 3))
    zeros = jnp.zeros((8, LANES - 32), F32)
    for r in range(NR):
        lanes = slice(16 * r, 16 * (r + 1))
        e_ref[r] = jnp.concatenate([mixed[:8, lanes], mixed[8:, lanes], zeros], axis=-1)


def fold(r):
    return pl.pallas_call(
        fold_kernel,
        out_shape=(
            jax.ShapeDtypeStruct((NJ, NAB), F32),
            jax.ShapeDtypeStruct((NR, 8, LANES), F32),
        ),
        name="fold",
    )(r)


def finish_kernel(d_ref, m_ref, rest_ref, den_ref, out_ref):
    halves = [
        jnp.concatenate([m_ref[r, :, 16 * h : 16 * (h + 1)] for r in range(NR)], axis=-1)
        for h in range(2)
    ]
    mirror = permute_lanes(
        jnp.concatenate(halves, axis=0), lambda n: ((n >> 2) & 15) * 16 + (n & 3) * 4 + (n >> 6)
    )
    value = (d_ref[...] + mirror + rest_ref[...]) / den_ref[...]
    for a in range(4):
        out_ref[:, a, :] = value[:, 64 * a : 64 * (a + 1)]


def finish(d, m, rest, den):
    return pl.pallas_call(
        finish_kernel, out_shape=jax.ShapeDtypeStruct((NJ, 4, 64), F32), name="finish"
    )(d, m, rest, den)


AXES = ("row", "col")


def moves(dz=0, dy=0):
    pairs = []
    for z in range(NZ):
        for h in range(2):
            for k in range(NC):
                to = ((z + dz) % NZ * 2 + (h ^ dy)) * NC + k
                pairs.append(((z * 2 + h) * NC + k, to))
    return pairs


UP, DOWN, ACROSS = moves(dz=1), moves(dz=-1), moves(dy=1)


def send(x, where):
    return lax.ppermute(x, AXES, where)


def on_device(amplitudes, integrals, rest, occ_energy, vir_energy):
    row = lax.axis_index("row")
    col = lax.axis_index("col")
    a0, b0 = pack_t(jnp.transpose(amplitudes, (0, 2, 1, 3))[0])
    v = jnp.transpose(integrals, (0, 2, 1, 3))
    vah, val = pack_va(v)
    vbh, vbl = pack_vb(v)

    bx = send(b0, ACROSS)
    au, ad, yu, yd = [a0], [a0], [send(a0, ACROSS)], [None]
    bb = jnp.stack([b0, bx])
    bu, bd = [bb], [bb]
    for _ in range(3):
        au.append(send(au[-1], UP))
        ad.append(send(ad[-1], DOWN))
        bu.append(send(bu[-1], UP))
        bd.append(send(bd[-1], DOWN))
        yu.append(send(au[-1], ACROSS))
        yd.append(send(ad[-1], ACROSS))
    a4 = send(au[3], UP)
    a4x = send(yd[3], DOWN)
    b4 = send(bu[3][0], UP)
    b4x = send(bd[3][1], DOWN)

    blocks, where, pairs = [au[0], yu[0]], [(0, 0), (0, 1)], [bb]
    for s in (1, 2, 3):
        blocks += [au[s], yu[s], ad[s], yd[s]]
        where += [(-s, 0), (-s, 1), (s, 0), (s, 1)]
        pairs += [bu[s], bd[s]]
    blocks += [a4, a4x]
    where += [(4, 0), (4, 1)]
    n1 = 10
    pa1 = dot_a(blocks[:n1], vah, val)
    pa2 = dot_a(blocks[n1:], vah, val)
    pb = dot_b(pairs[:5], NJ * n1, vbh, vbl)
    partial = last(row.reshape(1), where, n1, pairs[5:] + [b4, b4x], vbh, vbl, pa1, pa2, pb)

    received = lax.all_to_all(partial, "col", 0, 0, tiled=True)
    direct, messages = fold(received)
    mirror = lax.all_to_all(messages, "row", 0, 0, tiled=True)

    vir_local = lax.dynamic_slice_in_dim(vir_energy, row * 4, 4, 0)
    occ_local = lax.dynamic_slice_in_dim(occ_energy, col, 1, 0)
    den = (
        vir_local[None, :, None] + vir_energy[None, None, :] - occ_local[:, None, None]
        - occ_energy[:, None, None]
    )
    out = finish(direct, mirror, rest.reshape(NJ, NAB), den.reshape(NJ, NAB))
    return out[None]


def solution(mesh):
    in_specs = (
        P("row", None, "col", None),
        P("row", None, "col", None),
        P("col", None, "row", None),
        P(),
        P(),
    )

    return jax.shard_map(
        on_device, mesh=mesh, in_specs=in_specs, out_specs=P("col", None, "row", None), check_vma=False
    )
```

```python
import jax
import jax.numpy as jnp
from jax import lax
from jax.experimental import pallas as pl
from jax.experimental.pallas import tpu as pltpu
from jax.sharding import PartitionSpec as P


NR, NC = 16, 16
NZ = 8
ND = 400
LANES = 128
NJ, NAB = 16, 256
TA, TB = 50, 29
F32, BF16 = jnp.float32, jnp.bfloat16
LAST_OUT = pltpu.VMEM

VMEM = pl.BlockSpec(memory_space=pltpu.VMEM)


def params(mib):
    return pltpu.CompilerParams(vmem_limit_bytes=mib << 20)


def on_chip(x):
    return pltpu.with_memory_space_constraint(x, pltpu.VMEM)


def rows_of_rest(x, n):
    parts = [x(c) for c in range(n)]
    if n < 8:
        parts.append(jnp.zeros(parts[0].shape[:-1] + (LANES - 16 * n,), F32))
    return jnp.concatenate(parts, axis=-1)


def pack_t_kernel(row_ref, t_ref, a_ref, b_ref):
    for ref, at, c0, n in ((a_ref, 0, 0, 8), (a_ref, 25, 8, 8), (b_ref, 0, 16, 8), (b_ref, 25, 24, 1)):
        for c in range(n):
            for s in range(3):
                ref[at + 3 * c + s] = t_ref[c0 + c, :, LANES * s : LANES * (s + 1)]
        ref[at + 3 * n] = rows_of_rest(lambda c: t_ref[c0 + c, :, 384:400], n)


def pack_t(row, t):
    return pl.pallas_call(
        pack_t_kernel,
        in_specs=[pl.BlockSpec(memory_space=pltpu.SMEM), VMEM],
        out_specs=(VMEM, VMEM),
        out_shape=(pltpu.VMEM((TA, NJ, LANES), F32), pltpu.VMEM((TB, NJ, LANES), F32)),
        compiler_params=params(4),
        name="pack_t",
    )(row, t)


def split(x):
    hi = x.astype(BF16)
    return hi, (x - hi.astype(F32)).astype(BF16)


def pack_v_group(v_ref, h_ref, l_ref, at, n):
    for c in range(n):
        for s in range(3):
            t = at + 3 * c + s
            h_ref[t], l_ref[t] = split(v_ref[c, :, LANES * s : LANES * (s + 1)])
    t = at + 3 * n
    h_ref[t], l_ref[t] = split(rows_of_rest(lambda c: v_ref[c, :, 384:400], n))


def rows_64(at):
    return pl.ds(pl.multiple_of(at * 64, 64), 64)


def pack_va_kernel(v_ref, h_ref, l_ref):
    tiles, rows = pl.ds(pl.program_id(0) * 25, 25), rows_64(pl.program_id(1))
    pack_v_group(v_ref, h_ref.at[tiles, rows], l_ref.at[tiles, rows], 0, 8)


def pack_vb_kernel(v_ref, w_ref, h_ref, l_ref):
    rows = rows_64(pl.program_id(0))
    pack_v_group(v_ref, h_ref.at[:, rows], l_ref.at[:, rows], 0, 8)
    pack_v_group(w_ref, h_ref.at[:, rows], l_ref.at[:, rows], 25, 1)


def pack_va(v):
    out = pltpu.VMEM((TA, NAB, LANES), BF16)
    return pl.pallas_call(
        pack_va_kernel,
        grid=(2, 4),
        in_specs=[pl.BlockSpec((None, 8, 64, ND), lambda g, a: (a, g, 0, 0))],
        out_specs=(VMEM, VMEM),
        out_shape=(out, out),
        compiler_params=params(8),
        name="pack_va",
    )(v)


def pack_vb(v):
    out = pltpu.VMEM((TB, NAB, LANES), BF16)
    return pl.pallas_call(
        pack_vb_kernel,
        grid=(4,),
        in_specs=[
            pl.BlockSpec((None, 8, 64, ND), lambda a: (a, 2, 0, 0)),
            pl.BlockSpec((None, 1, 64, ND), lambda a: (a, 24, 0, 0)),
        ],
        out_specs=(VMEM, VMEM),
        out_shape=(out, out),
        compiler_params=params(8),
        name="pack_vb",
    )(v, v)


def product(t_refs, vh_ref, vl_ref, first, n):
    cat = lambda ref: jnp.concatenate([ref[first + t] for t in range(n)], axis=-1)
    hi, lo = split(jnp.concatenate([cat(r) for r in t_refs], axis=0))
    vh, vl = cat(vh_ref), cat(vl_ref)
    dims = (((1,), (1,)), ((), ()))
    both = lax.dot_general(jnp.concatenate([hi, lo], axis=0), vh, dims, preferred_element_type=F32)
    m = hi.shape[0]
    return both[:m] + both[m:] + lax.dot_general(hi, vl, dims, preferred_element_type=F32)


def product_b(refs, vh, vl):
    total = product(refs, vh, vl, 0, 6)
    for first, n in ((6, 6), (12, 6), (18, 6), (24, 5)):
        total += product(refs, vh, vl, first, n)
    return total


def dot_a_kernel(*refs):
    *t_refs, vh, vl, out = refs
    step = lambda g: product(t_refs, vh, vl, g * 10, 10)
    out[...] = lax.fori_loop(1, TA // 10, lambda g, total: total + step(g), step(0))


def dot(kernel, blocks, vh, vl):
    args = [on_chip(x) for x in (*blocks, vh, vl)]
    return pl.pallas_call(
        kernel,
        in_specs=[VMEM] * len(args),
        out_specs=VMEM,
        out_shape=pltpu.VMEM((NJ * len(blocks), NAB), F32),
        compiler_params=params(8),
    )(*args)


def dot_b_kernel(*refs):
    *t_refs, vh, vl, out = refs
    out[...] = product_b(t_refs, vh, vl)


def absolute_row(row, dz, dy):
    return (((row >> 1) + dz) & (NZ - 1)) * 2 + ((row & 1) ^ dy)


def last_kernel(where, row_ref, *refs):
    *t_refs, vh, vl, pa1, pa2, pb, out, left, right = refs
    new = product_b(t_refs, vh, vl)
    row = row_ref[0]
    n_a, n_b = pa1.shape[0] // NJ, pb.shape[0] // NJ
    part = lambda x, q: x[NJ * q : NJ * (q + 1), :]
    for q, (dz, dy) in enumerate(where):
        block = part(pa1, q) if q < n_a else part(pa2, q - n_a)
        block += part(pb, q) if q < n_b else part(new, q - n_b)
        at = pl.ds(pl.multiple_of(absolute_row(row, dz, dy) * NJ, NJ), NJ)
        left[at, :] = block[:, :LANES]
        right[at, :] = block[:, LANES:]
    for k in range(NC):
        for ref, lanes in ((left, slice(0, LANES)), (right, slice(LANES, NAB))):
            out[k, :NJ, lanes] = ref[NJ * k : NJ * (k + 1), :]
            out[k, NJ:, lanes] = ref[pl.ds(k, NJ, stride=NJ), :]


def last(row, where, blocks, vh, vl, pa1, pa2, pb):
    args = [on_chip(x) for x in (*blocks, vh, vl, pa1, pa2, pb)]
    return pl.pallas_call(
        lambda *refs: last_kernel(where, *refs),
        in_specs=[pl.BlockSpec(memory_space=pltpu.SMEM)] + [VMEM] * len(args),
        out_specs=VMEM,
        out_shape=LAST_OUT((NC, 2 * NJ, NAB), F32),
        scratch_shapes=[pltpu.VMEM((NAB, LANES), F32)] * 2,
        compiler_params=params(8),
        name="last",
    )(row, *args)


def permute_lanes(x, source):
    lane = lax.broadcasted_iota(jnp.int32, (NAB, NAB), 1)
    one_hot = (lax.broadcasted_iota(jnp.int32, (NAB, NAB), 0) == source(lane)).astype(BF16)
    p1, r1 = x.astype(BF16), x - x.astype(BF16).astype(F32)
    p2 = r1.astype(BF16)
    p3 = (r1 - p2.astype(F32)).astype(BF16)
    y = jnp.dot(jnp.concatenate([p1, p2, p3], axis=0), one_hot, preferred_element_type=F32)
    m = x.shape[0]
    return y[:m] + y[m : 2 * m] + y[2 * m :]


def fold_kernel(r_ref, d_ref, e_ref):
    total = r_ref[0]
    for k in range(1, NC):
        total += r_ref[k]
    d_ref[...] = total[:NJ]
    mixed = permute_lanes(total[NJ:], lambda n: ((n >> 2) & 3) * 64 + (n >> 4) * 4 + (n & 3))
    zeros = jnp.zeros((8, LANES - 32), F32)
    for r in range(NR):
        lanes = slice(16 * r, 16 * (r + 1))
        e_ref[r] = jnp.concatenate([mixed[:8, lanes], mixed[8:, lanes], zeros], axis=-1)


def fold(r):
    return pl.pallas_call(
        fold_kernel,
        in_specs=[VMEM],
        out_specs=(VMEM, VMEM),
        out_shape=(pltpu.VMEM((NJ, NAB), F32), LAST_OUT((NR, 8, LANES), F32)),
        compiler_params=params(4),
        name="fold",
    )(on_chip(r))


def finish_kernel(d_ref, m_ref, rest_ref, den_ref, out_ref):
    halves = [
        jnp.concatenate([m_ref[r, :, 16 * h : 16 * (h + 1)] for r in range(NR)], axis=-1)
        for h in range(2)
    ]
    mirror = permute_lanes(
        jnp.concatenate(halves, axis=0), lambda n: ((n >> 2) & 15) * 16 + (n & 3) * 4 + (n >> 6)
    )
    value = (d_ref[...] + mirror + rest_ref[...]) / den_ref[...]
    for a in range(4):
        out_ref[:, a, :] = value[:, 64 * a : 64 * (a + 1)]


def finish(d, m, rest, den):
    args = [on_chip(x) for x in (d, m, rest, den)]
    return pl.pallas_call(
        finish_kernel,
        in_specs=[VMEM] * 4,
        out_specs=VMEM,
        out_shape=jax.ShapeDtypeStruct((NJ, 4, 64), F32),
        compiler_params=params(4),
        name="finish",
    )(*args)


AXES = ("row", "col")


def moves(dz=0, dy=0):
    pairs = []
    for z in range(NZ):
        for h in range(2):
            for k in range(NC):
                to = ((z + dz) % NZ * 2 + (h ^ dy)) * NC + k
                pairs.append(((z * 2 + h) * NC + k, to))
    return pairs


UP, DOWN, ACROSS = moves(dz=1), moves(dz=-1), moves(dy=1)


def send(x, where):
    return lax.ppermute(x, AXES, where)


def on_device(amplitudes, integrals, rest, occ_energy, vir_energy):
    row = lax.axis_index("row")
    col = lax.axis_index("col")
    row_1 = row.reshape(1)
    a0, b0 = pack_t(row_1, jnp.transpose(amplitudes, (0, 2, 1, 3))[0])
    v = jnp.transpose(integrals, (0, 2, 1, 3))
    v = pltpu.with_memory_space_constraint(v, pltpu.HBM)
    vah, val = pack_va(v)
    vbh, vbl = pack_vb(v)

    au, ad, yu, yd = [a0], [a0], [send(a0, ACROSS)], [None]
    bx = send(b0, ACROSS)
    bu, bd, cu, cd = [b0], [b0], [bx], [bx]
    for _ in range(3):
        for chain, way in (
            (au, UP), (ad, DOWN), (bu, UP), (bd, DOWN),
            (cu, UP), (cd, DOWN),
        ):
            chain.append(send(chain[-1], way))
        yu.append(send(au[-1], ACROSS))
        yd.append(send(ad[-1], ACROSS))
    a4 = send(au[3], UP)
    a4x = send(yd[3], DOWN)
    b4 = send(bu[3], UP)
    c4 = send(cd[3], DOWN)

    a_all, b_all, where = [a0, yu[0]], [b0, bx], [(0, 0), (0, 1)]
    for s in (1, 2, 3):
        a_all += [au[s], yu[s], ad[s], yd[s]]
        b_all += [bu[s], cu[s], bd[s], cd[s]]
        where += [(-s, 0), (-s, 1), (s, 0), (s, 1)]
    a_all += [a4, a4x]
    b_all += [b4, c4]
    where += [(4, 0), (4, 1)]
    pa1 = dot(dot_a_kernel, a_all[:N_A], vah, val)
    pa2 = dot(dot_a_kernel, a_all[N_A:], vah, val)
    pb = dot(dot_b_kernel, b_all[:N_B], vbh, vbl)
    partial = last(row_1, where, b_all[N_B:], vbh, vbl, pa1, pa2, pb)

    received = lax.all_to_all(partial, "col", 0, 0, tiled=True)
    direct, messages = fold(received)
    mirror = lax.all_to_all(messages, "row", 0, 0, tiled=True)

    vir_local = lax.dynamic_slice_in_dim(vir_energy, row * 4, 4, 0)
    occ_local = lax.dynamic_slice_in_dim(occ_energy, col, 1, 0)
    den = (
        vir_local[None, :, None] + vir_energy[None, None, :] - occ_local[:, None, None]
        - occ_energy[:, None, None]
    )
    out = finish(direct, mirror, rest.reshape(NJ, NAB), den.reshape(NJ, NAB))
    return out[None]


N_A, N_B = 14, 10


def solution(mesh):
    in_specs = (
        P("row", None, "col", None),
        P("row", None, "col", None),
        P("col", None, "row", None),
        P(),
        P(),
    )

    return jax.shard_map(
        on_device, mesh=mesh, in_specs=in_specs, out_specs=P("col", None, "row", None), check_vma=False
    )
```

```python
import jax
import jax.numpy as jnp
from jax import lax
from jax.experimental import pallas as pl
from jax.experimental.pallas import tpu as pltpu
from jax.sharding import PartitionSpec as P


NR, NC = 16, 16
NZ = 8
ND = 400
LANES = 128
NJ, NAB = 16, 256
TA, TB = 52, 27
F32, BF16 = jnp.float32, jnp.bfloat16
LAST_OUT = pltpu.VMEM

VMEM = pl.BlockSpec(memory_space=pltpu.VMEM)


def params(mib):
    return pltpu.CompilerParams(vmem_limit_bytes=mib << 20)


def on_chip(x):
    return pltpu.with_memory_space_constraint(x, pltpu.VMEM)


def rows_of_rest(x, n):
    parts = [x(c) for c in range(n)]
    if n < 8:
        parts.append(jnp.zeros(parts[0].shape[:-1] + (LANES - 16 * n,), F32))
    return jnp.concatenate(parts, axis=-1)


def pack_t_kernel(at_ref, t_ref, a_ref, b_ref):
    for ref, at, c0 in ((a_ref, 0, 0), (a_ref, 25, 8), (b_ref, 0, 16)):
        for c in range(8):
            for s in range(3):
                ref[at + 3 * c + s] = t_ref[c0 + c, :, LANES * s : LANES * (s + 1)]
        ref[at + 24] = rows_of_rest(lambda c: t_ref[c0 + c, :, 384:400], 8)
    a_ref[50] = t_ref[24, :, :LANES]
    a_ref[51] = t_ref[24, :, LANES : 2 * LANES]
    b_ref[25] = t_ref[24, :, 2 * LANES : 384]
    b_ref[26] = rows_of_rest(lambda c: t_ref[24, :, 384:400], 1)


def pack_t(at, t):
    return pl.pallas_call(
        pack_t_kernel,
        in_specs=[pl.BlockSpec(memory_space=pltpu.SMEM), VMEM],
        out_specs=(VMEM, VMEM),
        out_shape=(pltpu.VMEM((TA, NJ, LANES), F32), pltpu.VMEM((TB, NJ, LANES), F32)),
        compiler_params=params(4),
        name="pack_t",
    )(at, t)


def split(x):
    hi = x.astype(BF16)
    return hi, (x - hi.astype(F32)).astype(BF16)


def pack_v_group(v_ref, h_ref, l_ref):
    for c in range(8):
        for s in range(3):
            t = 3 * c + s
            h_ref[t], l_ref[t] = split(v_ref[c, :, LANES * s : LANES * (s + 1)])
    h_ref[24], l_ref[24] = split(rows_of_rest(lambda c: v_ref[c, :, 384:400], 8))


def rows_64(at):
    return pl.ds(pl.multiple_of(at * 64, 64), 64)


def pack_va_kernel(v_ref, w_ref, h_ref, l_ref):
    group, rows = pl.program_id(0), rows_64(pl.program_id(1))
    tiles = pl.ds(group * 25, 25)
    pack_v_group(v_ref, h_ref.at[tiles, rows], l_ref.at[tiles, rows])

    @pl.when(group == 1)
    def _():
        for s in range(2):
            tile = split(w_ref[0, :, LANES * s : LANES * (s + 1)])
            h_ref[50 + s, rows, :], l_ref[50 + s, rows, :] = tile


def pack_vb_kernel(v_ref, w_ref, h_ref, l_ref):
    rows = rows_64(pl.program_id(0))
    pack_v_group(v_ref, h_ref.at[:, rows], l_ref.at[:, rows])
    h_ref[25, rows, :], l_ref[25, rows, :] = split(w_ref[0, :, 2 * LANES : 384])
    h_ref[26, rows, :], l_ref[26, rows, :] = split(rows_of_rest(lambda c: w_ref[0, :, 384:400], 1))


def pack_va(v):
    out = pltpu.VMEM((TA, NAB, LANES), BF16)
    return pl.pallas_call(
        pack_va_kernel,
        grid=(2, 4),
        in_specs=[
            pl.BlockSpec((None, 8, 64, ND), lambda g, a: (a, g, 0, 0)),
            pl.BlockSpec((None, 1, 64, ND), lambda g, a: (a, 24, 0, 0)),
        ],
        out_specs=(VMEM, VMEM),
        out_shape=(out, out),
        compiler_params=params(8),
        name="pack_va",
    )(v, v)


def pack_vb(v):
    out = pltpu.VMEM((TB, NAB, LANES), BF16)
    return pl.pallas_call(
        pack_vb_kernel,
        grid=(4,),
        in_specs=[
            pl.BlockSpec((None, 8, 64, ND), lambda a: (a, 2, 0, 0)),
            pl.BlockSpec((None, 1, 64, ND), lambda a: (a, 24, 0, 0)),
        ],
        out_specs=(VMEM, VMEM),
        out_shape=(out, out),
        compiler_params=params(8),
        name="pack_vb",
    )(v, v)


def product(t_refs, vh_ref, vl_ref, first, n):
    cat = lambda ref: jnp.concatenate([ref[first + t] for t in range(n)], axis=-1)
    hi, lo = split(jnp.concatenate([cat(r) for r in t_refs], axis=0))
    vh, vl = cat(vh_ref), cat(vl_ref)
    dims = (((1,), (1,)), ((), ()))
    both = lax.dot_general(jnp.concatenate([hi, lo], axis=0), vh, dims, preferred_element_type=F32)
    m = hi.shape[0]
    return both[:m] + both[m:] + lax.dot_general(hi, vl, dims, preferred_element_type=F32)


def product_b(refs, vh, vl):
    total = product(refs, vh, vl, 0, 6)
    for first, n in ((6, 6), (12, 6), (18, 6), (24, 3)):
        total += product(refs, vh, vl, first, n)
    return total


def dot_a_kernel(*refs):
    *t_refs, vh, vl, out = refs
    step = lambda g: product(t_refs, vh, vl, g * 10, 10)
    total = lax.fori_loop(1, TA // 10, lambda g, total: total + step(g), step(0))
    out[...] = total + product(t_refs, vh, vl, 50, 2)


def dot(kernel, blocks, vh, vl):
    args = [on_chip(x) for x in (*blocks, vh, vl)]
    return pl.pallas_call(
        kernel,
        in_specs=[VMEM] * len(args),
        out_specs=VMEM,
        out_shape=pltpu.VMEM((NJ * len(blocks), NAB), F32),
        compiler_params=params(8),
    )(*args)


def dot_b_kernel(*refs):
    *t_refs, vh, vl, out = refs
    out[...] = product_b(t_refs, vh, vl)


def absolute_row(row, dz, dy):
    return (((row >> 1) + dz) & (NZ - 1)) * 2 + ((row & 1) ^ dy)


def last_kernel(where, at_ref, *refs):
    *t_refs, vh, vl, pa1, pa2, pb, keep, give, left, right = refs
    new = product_b(t_refs, vh, vl)
    row, core = at_ref[0], at_ref[1] & 1
    n_a, n_b = pa1.shape[0] // NJ, pb.shape[0] // NJ
    part = lambda x, q: x[NJ * q : NJ * (q + 1), :]
    for q, (dz, dy) in enumerate(where):
        block = part(pa1, q) if q < n_a else part(pa2, q - n_a)
        block += part(pb, q) if q < n_b else part(new, q - n_b)
        at = pl.ds(pl.multiple_of(absolute_row(row, dz, dy) * NJ, NJ), NJ)
        left[at, :] = block[:, :LANES]
        right[at, :] = block[:, LANES:]
    for other, out in enumerate((keep, give)):
        for m in range(NC // 2):
            k = 2 * m + (core ^ other)
            for ref, lanes in ((left, slice(0, LANES)), (right, slice(LANES, NAB))):
                out[m, :NJ, lanes] = ref[pl.ds(pl.multiple_of(k * NJ, NJ), NJ), :]
                out[m, NJ:, lanes] = ref[pl.ds(k, NJ, stride=NJ), :]


def last(at, where, blocks, vh, vl, pa1, pa2, pb):
    out = pltpu.VMEM((NC // 2, 2 * NJ, NAB), F32)
    args = [on_chip(x) for x in (*blocks, vh, vl, pa1, pa2, pb)]
    return pl.pallas_call(
        lambda *refs: last_kernel(where, *refs),
        in_specs=[pl.BlockSpec(memory_space=pltpu.SMEM)] + [VMEM] * len(args),
        out_specs=(VMEM, VMEM),
        out_shape=(out, out),
        scratch_shapes=[pltpu.VMEM((NAB, LANES), F32)] * 2,
        compiler_params=params(8),
        name="last",
    )(at, *args)


def permute_lanes(x, source):
    lane = lax.broadcasted_iota(jnp.int32, (NAB, NAB), 1)
    one_hot = (lax.broadcasted_iota(jnp.int32, (NAB, NAB), 0) == source(lane)).astype(BF16)
    p1, r1 = x.astype(BF16), x - x.astype(BF16).astype(F32)
    p2 = r1.astype(BF16)
    p3 = (r1 - p2.astype(F32)).astype(BF16)
    y = jnp.dot(jnp.concatenate([p1, p2, p3], axis=0), one_hot, preferred_element_type=F32)
    m = x.shape[0]
    return y[:m] + y[m : 2 * m] + y[2 * m :]


def fold_kernel(r_ref, d_ref, e_ref):
    total = r_ref[0]
    for k in range(1, NC // 2):
        total += r_ref[k]
    d_ref[...] = total[:NJ]
    mixed = permute_lanes(total[NJ:], lambda n: ((n >> 2) & 3) * 64 + (n >> 4) * 4 + (n & 3))
    zeros = jnp.zeros((8, LANES - 32), F32)
    for r in range(NR):
        lanes = slice(16 * r, 16 * (r + 1))
        e_ref[r] = jnp.concatenate([mixed[:8, lanes], mixed[8:, lanes], zeros], axis=-1)


def fold(r):
    return pl.pallas_call(
        fold_kernel,
        in_specs=[VMEM],
        out_specs=(VMEM, VMEM),
        out_shape=(pltpu.VMEM((NJ, NAB), F32), LAST_OUT((NR, 8, LANES), F32)),
        compiler_params=params(4),
        name="fold",
    )(on_chip(r))


def finish_kernel(d_ref, m_ref, rest_ref, den_ref, out_ref):
    halves = [
        jnp.concatenate([m_ref[r, :, 16 * h : 16 * (h + 1)] for r in range(NR)], axis=-1)
        for h in range(2)
    ]
    mirror = permute_lanes(
        jnp.concatenate(halves, axis=0), lambda n: ((n >> 2) & 15) * 16 + (n & 3) * 4 + (n >> 6)
    )
    value = (d_ref[...] + mirror + rest_ref[...]) / den_ref[...]
    for a in range(4):
        out_ref[:, a, :] = value[:, 64 * a : 64 * (a + 1)]


def finish(d, m, rest, den):
    args = [on_chip(x) for x in (d, m, rest, den)]
    return pl.pallas_call(
        finish_kernel,
        in_specs=[VMEM] * 4,
        out_specs=VMEM,
        out_shape=jax.ShapeDtypeStruct((NJ, 4, 64), F32),
        compiler_params=params(4),
        name="finish",
    )(*args)


AXES = ("row", "col")


def moves(dz=0, dy=0):
    pairs = []
    for z in range(NZ):
        for h in range(2):
            for k in range(NC):
                to = ((z + dz) % NZ * 2 + (h ^ dy)) * NC + k
                pairs.append(((z * 2 + h) * NC + k, to))
    return pairs


UP, DOWN, ACROSS = moves(dz=1), moves(dz=-1), moves(dy=1)
OTHER_CORE = [(i, i ^ 1) for i in range(NR * NC)]
SAME_CORE = [[r * NC + 2 * m + core for m in range(NC // 2)] for r in range(NR) for core in range(2)]


def send(x, where):
    return lax.ppermute(x, AXES, where)


def on_device(amplitudes, integrals, rest, occ_energy, vir_energy):
    row = lax.axis_index("row")
    col = lax.axis_index("col")
    at = jnp.stack([row, col])
    a0, b0 = pack_t(at, jnp.transpose(amplitudes, (0, 2, 1, 3))[0])
    v = jnp.transpose(integrals, (0, 2, 1, 3))
    v = pltpu.with_memory_space_constraint(v, pltpu.HBM)
    vah, val = pack_va(v)
    vbh, vbl = pack_vb(v)

    au, ad, yu, yd = [a0], [a0], [send(a0, ACROSS)], [None]
    bx = send(b0, ACROSS)
    bu, bd, cu, cd = [b0], [b0], [bx], [bx]
    for _ in range(3):
        for chain, way in (
            (au, UP), (ad, DOWN), (bu, UP), (bd, DOWN),
            (cu, UP), (cd, DOWN),
        ):
            chain.append(send(chain[-1], way))
        yu.append(send(au[-1], ACROSS))
        yd.append(send(ad[-1], ACROSS))
    a4 = send(au[3], UP)
    a4x = send(yd[3], DOWN)
    b4 = send(bu[3], UP)
    c4 = send(cd[3], DOWN)

    a_all, b_all, where = [a0, yu[0]], [b0, bx], [(0, 0), (0, 1)]
    for s in (1, 2):
        a_all += [au[s], yu[s], ad[s], yd[s]]
        b_all += [bu[s], cu[s], bd[s], cd[s]]
        where += [(-s, 0), (-s, 1), (s, 0), (s, 1)]
    a_all += [au[3], ad[3], yd[3], yu[3], a4, a4x]
    b_all += [bu[3], bd[3], cd[3], cu[3], b4, c4]
    where += [(-3, 0), (3, 0), (3, 1), (-3, 1), (4, 0), (4, 1)]
    pa1 = dot(dot_a_kernel, a_all[:N_A], vah, val)
    pa2 = dot(dot_a_kernel, a_all[N_A:], vah, val)
    pb = dot(dot_b_kernel, b_all[:N_B], vbh, vbl)
    keep, give = last(at, where, b_all[N_B:], vbh, vbl, pa1, pa2, pb)

    partial = keep + send(give, OTHER_CORE)
    received = lax.all_to_all(
        partial, AXES, 0, 0, axis_index_groups=SAME_CORE, tiled=True
    )
    direct, messages = fold(received)
    mirror = lax.all_to_all(messages, "row", 0, 0, tiled=True)

    vir_local = lax.dynamic_slice_in_dim(vir_energy, row * 4, 4, 0)
    occ_local = lax.dynamic_slice_in_dim(occ_energy, col, 1, 0)
    den = (
        vir_local[None, :, None] + vir_energy[None, None, :] - occ_local[:, None, None]
        - occ_energy[:, None, None]
    )
    out = finish(direct, mirror, rest.reshape(NJ, NAB), den.reshape(NJ, NAB))
    return out[None]


N_A, N_B = 13, 10


def solution(mesh):
    in_specs = (
        P("row", None, "col", None),
        P("row", None, "col", None),
        P("col", None, "row", None),
        P(),
        P(),
    )

    return jax.shard_map(
        on_device, mesh=mesh, in_specs=in_specs, out_specs=P("col", None, "row", None), check_vma=False
    )
```

```python
import jax
import jax.numpy as jnp
from jax import lax
from jax.experimental import pallas as pl
from jax.experimental.pallas import tpu as pltpu
from jax.sharding import PartitionSpec as P


NR, NC = 16, 16
NZ = 8
ND = 400
LANES = 128
NJ, NAB = 16, 256
TA, TB = 52, 27
F32, BF16 = jnp.float32, jnp.bfloat16
LAST_OUT = pltpu.VMEM

VMEM = pl.BlockSpec(memory_space=pltpu.VMEM)


def params(mib):
    return pltpu.CompilerParams(vmem_limit_bytes=mib << 20)


def on_chip(x):
    return pltpu.with_memory_space_constraint(x, pltpu.VMEM)


def rows_of_rest(x, n):
    parts = [x(c) for c in range(n)]
    if n < 8:
        parts.append(jnp.zeros(parts[0].shape[:-1] + (LANES - 16 * n,), F32))
    return jnp.concatenate(parts, axis=-1)


def pack_t_kernel(at_ref, t_ref, a_ref, b_ref):
    for ref, at, c0 in ((a_ref, 0, 0), (a_ref, 25, 8), (b_ref, 0, 16)):
        for c in range(8):
            for s in range(3):
                ref[at + 3 * c + s] = t_ref[c0 + c, :, LANES * s : LANES * (s + 1)]
        ref[at + 24] = rows_of_rest(lambda c: t_ref[c0 + c, :, 384:400], 8)
    a_ref[50] = t_ref[24, :, :LANES]
    a_ref[51] = t_ref[24, :, LANES : 2 * LANES]
    b_ref[25] = t_ref[24, :, 2 * LANES : 384]
    b_ref[26] = rows_of_rest(lambda c: t_ref[24, :, 384:400], 1)


def pack_t(at, t):
    return pl.pallas_call(
        pack_t_kernel,
        in_specs=[pl.BlockSpec(memory_space=pltpu.SMEM), VMEM],
        out_specs=(VMEM, VMEM),
        out_shape=(pltpu.VMEM((TA, NJ, LANES), F32), pltpu.VMEM((TB, NJ, LANES), F32)),
        compiler_params=params(4),
        name="pack_t",
    )(at, t)


def split(x):
    hi = x.astype(BF16)
    return hi, (x - hi.astype(F32)).astype(BF16)


def pack_v_group(v_ref, h_ref, l_ref):
    for c in range(8):
        for s in range(3):
            t = 3 * c + s
            h_ref[t], l_ref[t] = split(v_ref[c, :, LANES * s : LANES * (s + 1)])
    h_ref[24], l_ref[24] = split(rows_of_rest(lambda c: v_ref[c, :, 384:400], 8))


def rows_64(at):
    return pl.ds(pl.multiple_of(at * 64, 64), 64)


def pack_va_kernel(v_ref, w_ref, h_ref, l_ref):
    group, rows = pl.program_id(0), rows_64(pl.program_id(1))
    tiles = pl.ds(group * 25, 25)
    pack_v_group(v_ref, h_ref.at[tiles, rows], l_ref.at[tiles, rows])

    @pl.when(group == 1)
    def _():
        for s in range(2):
            tile = split(w_ref[0, :, LANES * s : LANES * (s + 1)])
            h_ref[50 + s, rows, :], l_ref[50 + s, rows, :] = tile


def pack_vb_kernel(v_ref, w_ref, h_ref, l_ref):
    rows = rows_64(pl.program_id(0))
    pack_v_group(v_ref, h_ref.at[:, rows], l_ref.at[:, rows])
    h_ref[25, rows, :], l_ref[25, rows, :] = split(w_ref[0, :, 2 * LANES : 384])
    h_ref[26, rows, :], l_ref[26, rows, :] = split(rows_of_rest(lambda c: w_ref[0, :, 384:400], 1))


def pack_va(v):
    out = pltpu.VMEM((TA, NAB, LANES), BF16)
    return pl.pallas_call(
        pack_va_kernel,
        grid=(2, 4),
        in_specs=[
            pl.BlockSpec((None, 8, 64, ND), lambda g, a: (a, g, 0, 0)),
            pl.BlockSpec((None, 1, 64, ND), lambda g, a: (a, 24, 0, 0)),
        ],
        out_specs=(VMEM, VMEM),
        out_shape=(out, out),
        compiler_params=params(8),
        name="pack_va",
    )(v, v)


def pack_vb(v):
    out = pltpu.VMEM((TB, NAB, LANES), BF16)
    return pl.pallas_call(
        pack_vb_kernel,
        grid=(4,),
        in_specs=[
            pl.BlockSpec((None, 8, 64, ND), lambda a: (a, 2, 0, 0)),
            pl.BlockSpec((None, 1, 64, ND), lambda a: (a, 24, 0, 0)),
        ],
        out_specs=(VMEM, VMEM),
        out_shape=(out, out),
        compiler_params=params(8),
        name="pack_vb",
    )(v, v)


def product(t_refs, vh_ref, vl_ref, first, n):
    cat = lambda ref: jnp.concatenate([ref[first + t] for t in range(n)], axis=-1)
    hi, lo = split(jnp.concatenate([cat(r) for r in t_refs], axis=0))
    vh, vl = cat(vh_ref), cat(vl_ref)
    dims = (((1,), (1,)), ((), ()))
    both = lax.dot_general(jnp.concatenate([hi, lo], axis=0), vh, dims, preferred_element_type=F32)
    m = hi.shape[0]
    return both[:m] + both[m:] + lax.dot_general(hi, vl, dims, preferred_element_type=F32)


def product_b(refs, vh, vl):
    total = product(refs, vh, vl, 0, 6)
    for first, n in ((6, 6), (12, 6), (18, 6), (24, 3)):
        total += product(refs, vh, vl, first, n)
    return total


def dot_a_kernel(*refs):
    *t_refs, vh, vl, out = refs
    step = lambda g: product(t_refs, vh, vl, g * 10, 10)
    total = lax.fori_loop(1, TA // 10, lambda g, total: total + step(g), step(0))
    out[...] = total + product(t_refs, vh, vl, 50, 2)


def dot(kernel, blocks, vh, vl):
    args = [on_chip(x) for x in (*blocks, vh, vl)]
    return pl.pallas_call(
        kernel,
        in_specs=[VMEM] * len(args),
        out_specs=VMEM,
        out_shape=pltpu.VMEM((NJ * len(blocks), NAB), F32),
        compiler_params=params(8),
    )(*args)


def dot_b_kernel(*refs):
    *t_refs, vh, vl, out = refs
    out[...] = product_b(t_refs, vh, vl)


def absolute_row(row, dz, dy):
    return (((row >> 1) + dz) & (NZ - 1)) * 2 + ((row & 1) ^ dy)


def last_kernel(where, at_ref, *refs):
    *t_refs, vh, vl, pa1, pa2, pb, keep, give, left, right = refs
    new = product_b(t_refs, vh, vl)
    row, core = at_ref[0], at_ref[1] & 1
    n_a, n_b = pa1.shape[0] // NJ, pb.shape[0] // NJ
    part = lambda x, q: x[NJ * q : NJ * (q + 1), :]
    for q, (dz, dy) in enumerate(where):
        block = part(pa1, q) if q < n_a else part(pa2, q - n_a)
        block += part(pb, q) if q < n_b else part(new, q - n_b)
        at = pl.ds(pl.multiple_of(absolute_row(row, dz, dy) * NJ, NJ), NJ)
        left[at, :] = block[:, :LANES]
        right[at, :] = block[:, LANES:]
    for other, out in enumerate((keep, give)):
        for m in range(NC // 2):
            k = 2 * m + (core ^ other)
            for ref, lanes in ((left, slice(0, LANES)), (right, slice(LANES, NAB))):
                out[(m - FIRST_CHIP) % 8, :NJ, lanes] = ref[pl.ds(pl.multiple_of(k * NJ, NJ), NJ), :]
                out[(m - FIRST_CHIP) % 8, NJ:, lanes] = ref[pl.ds(k, NJ, stride=NJ), :]


def last(at, where, blocks, vh, vl, pa1, pa2, pb):
    out = pltpu.VMEM((NC // 2, 2 * NJ, NAB), F32)
    args = [on_chip(x) for x in (*blocks, vh, vl, pa1, pa2, pb)]
    return pl.pallas_call(
        lambda *refs: last_kernel(where, *refs),
        in_specs=[pl.BlockSpec(memory_space=pltpu.SMEM)] + [VMEM] * len(args),
        out_specs=(VMEM, VMEM),
        out_shape=(out, out),
        scratch_shapes=[pltpu.VMEM((NAB, LANES), F32)] * 2,
        compiler_params=params(8),
        name="last",
    )(at, *args)


def permute_lanes(x, source):
    lane = lax.broadcasted_iota(jnp.int32, (NAB, NAB), 1)
    one_hot = (lax.broadcasted_iota(jnp.int32, (NAB, NAB), 0) == source(lane)).astype(BF16)
    p1, r1 = x.astype(BF16), x - x.astype(BF16).astype(F32)
    p2 = r1.astype(BF16)
    p3 = (r1 - p2.astype(F32)).astype(BF16)
    y = jnp.dot(jnp.concatenate([p1, p2, p3], axis=0), one_hot, preferred_element_type=F32)
    m = x.shape[0]
    return y[:m] + y[m : 2 * m] + y[2 * m :]


def fold_kernel(r_ref, d_ref, e_ref):
    total = r_ref[0]
    for k in range(1, NC // 2):
        total += r_ref[k]
    d_ref[...] = total[:NJ]
    mixed = permute_lanes(total[NJ:], lambda n: ((n >> 2) & 3) * 64 + (n >> 4) * 4 + (n & 3))
    zeros = jnp.zeros((8, LANES - 32), F32)
    for r in range(NR):
        lanes = slice(16 * r, 16 * (r + 1))
        e_ref[(r - FIRST_ROW) % NR] = jnp.concatenate([mixed[:8, lanes], mixed[8:, lanes], zeros], axis=-1)


def fold(r):
    return pl.pallas_call(
        fold_kernel,
        in_specs=[VMEM],
        out_specs=(VMEM, VMEM),
        out_shape=(pltpu.VMEM((NJ, NAB), F32), LAST_OUT((NR, 8, LANES), F32)),
        compiler_params=params(4),
        name="fold",
    )(on_chip(r))


def finish_kernel(d_ref, m_ref, rest_ref, den_ref, out_ref):
    halves = [
        jnp.concatenate([m_ref[(r - FIRST_ROW) % NR, :, 16 * h : 16 * (h + 1)] for r in range(NR)], axis=-1)
        for h in range(2)
    ]
    mirror = permute_lanes(
        jnp.concatenate(halves, axis=0), lambda n: ((n >> 2) & 15) * 16 + (n & 3) * 4 + (n >> 6)
    )
    value = (d_ref[...] + mirror + rest_ref[...]) / den_ref[...]
    for a in range(4):
        out_ref[:, a, :] = value[:, 64 * a : 64 * (a + 1)]


def finish(d, m, rest, den):
    args = [on_chip(x) for x in (d, m, rest, den)]
    return pl.pallas_call(
        finish_kernel,
        in_specs=[VMEM] * 4,
        out_specs=VMEM,
        out_shape=jax.ShapeDtypeStruct((NJ, 4, 64), F32),
        compiler_params=params(4),
        name="finish",
    )(*args)


AXES = ("row", "col")


def moves(dz=0, dy=0):
    pairs = []
    for z in range(NZ):
        for h in range(2):
            for k in range(NC):
                to = ((z + dz) % NZ * 2 + (h ^ dy)) * NC + k
                pairs.append(((z * 2 + h) * NC + k, to))
    return pairs


UP, DOWN, ACROSS = moves(dz=1), moves(dz=-1), moves(dy=1)
OTHER_CORE = [(i, i ^ 1) for i in range(NR * NC)]
FIRST_ROW = 9
SAME_COLUMN = [[(FIRST_ROW + m) % NR * NC + k for m in range(NR)] for k in range(NC)]
FIRST_CHIP = 5
SAME_CORE = [[r * NC + (FIRST_CHIP + m) % 8 * 2 + core for m in range(NC // 2)] for r in range(NR) for core in range(2)]


def send(x, where):
    return lax.ppermute(x, AXES, where)


def on_device(amplitudes, integrals, rest, occ_energy, vir_energy):
    row = lax.axis_index("row")
    col = lax.axis_index("col")
    at = jnp.stack([row, col])
    a0, b0 = pack_t(at, jnp.transpose(amplitudes, (0, 2, 1, 3))[0])
    v = jnp.transpose(integrals, (0, 2, 1, 3))
    v = pltpu.with_memory_space_constraint(v, pltpu.HBM)
    vah, val = pack_va(v)
    vbh, vbl = pack_vb(v)

    au, ad, yu, yd = [a0], [a0], [send(a0, ACROSS)], [None]
    bx = send(b0, ACROSS)
    bu, bd, cu, cd = [b0], [b0], [bx], [bx]
    for _ in range(3):
        for chain, way in (
            (au, UP), (ad, DOWN), (bu, UP), (bd, DOWN),
            (cu, UP), (cd, DOWN),
        ):
            chain.append(send(chain[-1], way))
        yu.append(send(au[-1], ACROSS))
        yd.append(send(ad[-1], ACROSS))
    a4 = send(au[3], UP)
    a4x = send(yd[3], DOWN)
    b4 = send(bu[3], UP)
    c4 = send(cd[3], DOWN)

    a_all, b_all, where = [a0, yu[0]], [b0, bx], [(0, 0), (0, 1)]
    for s in (1, 2):
        a_all += [au[s], yu[s], ad[s], yd[s]]
        b_all += [bu[s], cu[s], bd[s], cd[s]]
        where += [(-s, 0), (-s, 1), (s, 0), (s, 1)]
    a_all += [au[3], ad[3], yd[3], yu[3], a4, a4x]
    b_all += [bu[3], bd[3], cd[3], cu[3], b4, c4]
    where += [(-3, 0), (3, 0), (3, 1), (-3, 1), (4, 0), (4, 1)]
    pa1 = dot(dot_a_kernel, a_all[:N_A], vah, val)
    pa2 = dot(dot_a_kernel, a_all[N_A:], vah, val)
    pb = dot(dot_b_kernel, b_all[:N_B], vbh, vbl)
    keep, give = last(at, where, b_all[N_B:], vbh, vbl, pa1, pa2, pb)

    partial = keep + send(give, OTHER_CORE)
    received = lax.all_to_all(
        partial, AXES, 0, 0, axis_index_groups=SAME_CORE, tiled=True
    )
    direct, messages = fold(received)
    mirror = lax.all_to_all(messages, AXES, 0, 0, axis_index_groups=SAME_COLUMN, tiled=True)

    vir_local = lax.dynamic_slice_in_dim(vir_energy, row * 4, 4, 0)
    occ_local = lax.dynamic_slice_in_dim(occ_energy, col, 1, 0)
    den = (
        vir_local[None, :, None] + vir_energy[None, None, :] - occ_local[:, None, None]
        - occ_energy[:, None, None]
    )
    out = finish(direct, mirror, rest.reshape(NJ, NAB), den.reshape(NJ, NAB))
    return out[None]


N_A, N_B = 13, 10


def solution(mesh):
    in_specs = (
        P("row", None, "col", None),
        P("row", None, "col", None),
        P("col", None, "row", None),
        P(),
        P(),
    )

    return jax.shard_map(
        on_device, mesh=mesh, in_specs=in_specs, out_specs=P("col", None, "row", None), check_vma=False
    )
```

```python
import jax
import jax.numpy as jnp
from jax import lax
from jax.experimental import pallas as pl
from jax.experimental.pallas import tpu as pltpu
from jax.sharding import PartitionSpec as P


NR, NC = 16, 16
NZ = 8
ND = 400
LANES = 128
NJ, NAB = 16, 256
TA, TB = 52, 27
F32, BF16 = jnp.float32, jnp.bfloat16
LAST_OUT = pltpu.VMEM

VMEM = pl.BlockSpec(memory_space=pltpu.VMEM)


def params(mib):
    return pltpu.CompilerParams(vmem_limit_bytes=mib << 20)


def on_chip(x):
    return pltpu.with_memory_space_constraint(x, pltpu.VMEM)


def rows_of_rest(x, n):
    parts = [x(c) for c in range(n)]
    if n < 8:
        parts.append(jnp.zeros(parts[0].shape[:-1] + (LANES - 16 * n,), F32))
    return jnp.concatenate(parts, axis=-1)


def pack_t_kernel(at_ref, t_ref, a_ref, b_ref):
    for ref, at, c0 in ((a_ref, 0, 0), (a_ref, 25, 8), (b_ref, 0, 16)):
        for c in range(8):
            for s in range(3):
                ref[at + 3 * c + s] = t_ref[c0 + c, :, LANES * s : LANES * (s + 1)]
        ref[at + 24] = rows_of_rest(lambda c: t_ref[c0 + c, :, 384:400], 8)
    a_ref[50] = t_ref[24, :, :LANES]
    a_ref[51] = t_ref[24, :, LANES : 2 * LANES]
    b_ref[25] = t_ref[24, :, 2 * LANES : 384]
    b_ref[26] = rows_of_rest(lambda c: t_ref[24, :, 384:400], 1)


def pack_t(at, t):
    return pl.pallas_call(
        pack_t_kernel,
        in_specs=[pl.BlockSpec(memory_space=pltpu.SMEM), VMEM],
        out_specs=(VMEM, VMEM),
        out_shape=(pltpu.VMEM((TA, NJ, LANES), F32), pltpu.VMEM((TB, NJ, LANES), F32)),
        compiler_params=params(4),
        name="pack_t",
    )(at, t)


def split(x):
    hi = x.astype(BF16)
    return hi, (x - hi.astype(F32)).astype(BF16)


def pack_v_group(v_ref, h_ref, l_ref):
    for c in range(8):
        for s in range(3):
            t = 3 * c + s
            h_ref[t], l_ref[t] = split(v_ref[c, :, LANES * s : LANES * (s + 1)])
    h_ref[24], l_ref[24] = split(rows_of_rest(lambda c: v_ref[c, :, 384:400], 8))


def rows_64(at):
    return pl.ds(pl.multiple_of(at * 64, 64), 64)


def pack_va_kernel(v_ref, w_ref, h_ref, l_ref):
    group, rows = pl.program_id(0), rows_64(pl.program_id(1))
    tiles = pl.ds(group * 25, 25)
    pack_v_group(v_ref, h_ref.at[tiles, rows], l_ref.at[tiles, rows])

    @pl.when(group == 1)
    def _():
        for s in range(2):
            tile = split(w_ref[0, :, LANES * s : LANES * (s + 1)])
            h_ref[50 + s, rows, :], l_ref[50 + s, rows, :] = tile


def pack_vb_kernel(v_ref, w_ref, h_ref, l_ref):
    rows = rows_64(pl.program_id(0))
    pack_v_group(v_ref, h_ref.at[:, rows], l_ref.at[:, rows])
    h_ref[25, rows, :], l_ref[25, rows, :] = split(w_ref[0, :, 2 * LANES : 384])
    h_ref[26, rows, :], l_ref[26, rows, :] = split(rows_of_rest(lambda c: w_ref[0, :, 384:400], 1))


def pack_va(v):
    out = pltpu.VMEM((TA, NAB, LANES), BF16)
    return pl.pallas_call(
        pack_va_kernel,
        grid=(2, 4),
        in_specs=[
            pl.BlockSpec((None, 8, 64, ND), lambda g, a: (a, g, 0, 0)),
            pl.BlockSpec((None, 1, 64, ND), lambda g, a: (a, 24, 0, 0)),
        ],
        out_specs=(VMEM, VMEM),
        out_shape=(out, out),
        compiler_params=params(8),
        name="pack_va",
    )(v, v)


def pack_vb(v):
    out = pltpu.VMEM((TB, NAB, LANES), BF16)
    return pl.pallas_call(
        pack_vb_kernel,
        grid=(4,),
        in_specs=[
            pl.BlockSpec((None, 8, 64, ND), lambda a: (a, 2, 0, 0)),
            pl.BlockSpec((None, 1, 64, ND), lambda a: (a, 24, 0, 0)),
        ],
        out_specs=(VMEM, VMEM),
        out_shape=(out, out),
        compiler_params=params(8),
        name="pack_vb",
    )(v, v)


def product(t_refs, vh_ref, vl_ref, first, n):
    cat = lambda ref: jnp.concatenate([ref[first + t] for t in range(n)], axis=-1)
    hi, lo = split(jnp.concatenate([cat(r) for r in t_refs], axis=0))
    vh, vl = cat(vh_ref), cat(vl_ref)
    dims = (((1,), (1,)), ((), ()))
    both = lax.dot_general(jnp.concatenate([hi, lo], axis=0), vh, dims, preferred_element_type=F32)
    m = hi.shape[0]
    return both[:m] + both[m:] + lax.dot_general(hi, vl, dims, preferred_element_type=F32)


def product_b(refs, vh, vl):
    total = product(refs, vh, vl, 0, 6)
    for first, n in ((6, 6), (12, 6), (18, 6), (24, 3)):
        total += product(refs, vh, vl, first, n)
    return total


def product_a(refs, vh, vl):
    step = lambda g: product(refs, vh, vl, g * 10, 10)
    total = lax.fori_loop(1, TA // 10, lambda g, total: total + step(g), step(0))
    return total + product(refs, vh, vl, 50, 2)


def dot_a_kernel(*refs):
    *t_refs, vh, vl, out = refs
    out[...] = product_a(t_refs, vh, vl)


def dot(kernel, blocks, vh, vl):
    args = [on_chip(x) for x in (*blocks, vh, vl)]
    return pl.pallas_call(
        kernel,
        in_specs=[VMEM] * len(args),
        out_specs=VMEM,
        out_shape=pltpu.VMEM((NJ * len(blocks), NAB), F32),
        compiler_params=params(8),
    )(*args)


def dot_b_kernel(*refs):
    *t_refs, vh, vl, out = refs
    out[...] = product_b(t_refs, vh, vl)


def absolute_row(row, dz, dy):
    return (((row >> 1) + dz) & (NZ - 1)) * 2 + ((row & 1) ^ dy)


def last_kernel(where, at_ref, *refs):
    *t_refs, vah, val, vbh, vbl, pa1, pb, keep, give, left, right = refs
    n_late = len(where) - pa1.shape[0] // NJ
    new_a = product_a(t_refs[:n_late], vah, val)
    new_b = product_b(t_refs[n_late:], vbh, vbl)
    row, core = at_ref[0], at_ref[1] & 1
    n_a, n_b = pa1.shape[0] // NJ, pb.shape[0] // NJ
    part = lambda x, q: x[NJ * q : NJ * (q + 1), :]
    for q, (dz, dy) in enumerate(where):
        block = part(pa1, q) if q < n_a else part(new_a, q - n_a)
        block += part(pb, q) if q < n_b else part(new_b, q - n_b)
        at = pl.ds(pl.multiple_of(absolute_row(row, dz, dy) * NJ, NJ), NJ)
        left[at, :] = block[:, :LANES]
        right[at, :] = block[:, LANES:]
    for other, out in enumerate((keep, give)):
        for m in range(NC // 2):
            k = 2 * m + (core ^ other)
            for ref, lanes in ((left, slice(0, LANES)), (right, slice(LANES, NAB))):
                out[(m - FIRST_CHIP) % 8, :NJ, lanes] = ref[pl.ds(pl.multiple_of(k * NJ, NJ), NJ), :]
                out[(m - FIRST_CHIP) % 8, NJ:, lanes] = ref[pl.ds(k, NJ, stride=NJ), :]


def last(at, where, blocks, v, pa1, pb):
    out = pltpu.VMEM((NC // 2, 2 * NJ, NAB), F32)
    args = [on_chip(x) for x in (*blocks, *v, pa1, pb)]
    return pl.pallas_call(
        lambda *refs: last_kernel(where, *refs),
        in_specs=[pl.BlockSpec(memory_space=pltpu.SMEM)] + [VMEM] * len(args),
        out_specs=(VMEM, VMEM),
        out_shape=(out, out),
        scratch_shapes=[pltpu.VMEM((NAB, LANES), F32)] * 2,
        compiler_params=params(8),
        name="last",
    )(at, *args)


def permute_lanes(x, source):
    lane = lax.broadcasted_iota(jnp.int32, (NAB, NAB), 1)
    one_hot = (lax.broadcasted_iota(jnp.int32, (NAB, NAB), 0) == source(lane)).astype(BF16)
    p1, r1 = x.astype(BF16), x - x.astype(BF16).astype(F32)
    p2 = r1.astype(BF16)
    p3 = (r1 - p2.astype(F32)).astype(BF16)
    y = jnp.dot(jnp.concatenate([p1, p2, p3], axis=0), one_hot, preferred_element_type=F32)
    m = x.shape[0]
    return y[:m] + y[m : 2 * m] + y[2 * m :]


def fold_kernel(r_ref, d_ref, e_ref):
    total = r_ref[0]
    for k in range(1, NC // 2):
        total += r_ref[k]
    d_ref[...] = total[:NJ]
    mixed = permute_lanes(total[NJ:], lambda n: ((n >> 2) & 3) * 64 + (n >> 4) * 4 + (n & 3))
    zeros = jnp.zeros((8, LANES - 32), F32)
    for r in range(NR):
        lanes = slice(16 * r, 16 * (r + 1))
        e_ref[(r - FIRST_ROW) % NR] = jnp.concatenate([mixed[:8, lanes], mixed[8:, lanes], zeros], axis=-1)


def fold(r):
    return pl.pallas_call(
        fold_kernel,
        in_specs=[VMEM],
        out_specs=(VMEM, VMEM),
        out_shape=(pltpu.VMEM((NJ, NAB), F32), LAST_OUT((NR, 8, LANES), F32)),
        compiler_params=params(4),
        name="fold",
    )(on_chip(r))


def finish_kernel(d_ref, m_ref, rest_ref, den_ref, out_ref):
    halves = [
        jnp.concatenate([m_ref[(r - FIRST_ROW) % NR, :, 16 * h : 16 * (h + 1)] for r in range(NR)], axis=-1)
        for h in range(2)
    ]
    mirror = permute_lanes(
        jnp.concatenate(halves, axis=0), lambda n: ((n >> 2) & 15) * 16 + (n & 3) * 4 + (n >> 6)
    )
    value = (d_ref[...] + mirror + rest_ref[...]) / den_ref[...]
    for a in range(4):
        out_ref[:, a, :] = value[:, 64 * a : 64 * (a + 1)]


def finish(d, m, rest, den):
    args = [on_chip(x) for x in (d, m, rest, den)]
    return pl.pallas_call(
        finish_kernel,
        in_specs=[VMEM] * 4,
        out_specs=VMEM,
        out_shape=jax.ShapeDtypeStruct((NJ, 4, 64), F32),
        compiler_params=params(4),
        name="finish",
    )(*args)


AXES = ("row", "col")


def moves(dz=0, dy=0):
    pairs = []
    for z in range(NZ):
        for h in range(2):
            for k in range(NC):
                to = ((z + dz) % NZ * 2 + (h ^ dy)) * NC + k
                pairs.append(((z * 2 + h) * NC + k, to))
    return pairs


UP, DOWN, ACROSS = moves(dz=1), moves(dz=-1), moves(dy=1)
OTHER_CORE = [(i, i ^ 1) for i in range(NR * NC)]
FIRST_ROW = 9
SAME_COLUMN = [[(FIRST_ROW + m) % NR * NC + k for m in range(NR)] for k in range(NC)]
FIRST_CHIP = 5
SAME_CORE = [[r * NC + (FIRST_CHIP + m) % 8 * 2 + core for m in range(NC // 2)] for r in range(NR) for core in range(2)]


def send(x, where):
    return lax.ppermute(x, AXES, where)


def on_device(amplitudes, integrals, rest, occ_energy, vir_energy):
    row = lax.axis_index("row")
    col = lax.axis_index("col")
    at = jnp.stack([row, col])
    t = jnp.transpose(amplitudes, (0, 2, 1, 3))[0]
    a0, b0 = pack_t(at, pltpu.with_memory_space_constraint(t, pltpu.HBM))
    v = jnp.transpose(integrals, (0, 2, 1, 3))
    v = pltpu.with_memory_space_constraint(v, pltpu.HBM)
    vah, val = pack_va(v)
    vbh, vbl = pack_vb(v)

    au, ad, yu, yd = [a0], [a0], [send(a0, ACROSS)], [None]
    bx = send(b0, ACROSS)
    bu, bd, cu, cd = [b0], [b0], [bx], [bx]
    for _ in range(3):
        for chain, way in (
            (au, UP), (ad, DOWN), (bu, UP), (bd, DOWN),
            (cu, UP), (cd, DOWN),
        ):
            chain.append(send(chain[-1], way))
        yu.append(send(au[-1], ACROSS))
        yd.append(send(ad[-1], ACROSS))
    a4 = send(au[3], UP)
    a4x = send(yd[3], DOWN)
    b4 = send(bu[3], UP)
    c4 = send(cd[3], DOWN)

    a_all, b_all, where = [a0, yu[0]], [b0, bx], [(0, 0), (0, 1)]
    for s in (1, 2):
        a_all += [au[s], yu[s], ad[s], yd[s]]
        b_all += [bu[s], cu[s], bd[s], cd[s]]
        where += [(-s, 0), (-s, 1), (s, 0), (s, 1)]
    a_all += [au[3], ad[3], yd[3], yu[3], a4, a4x]
    b_all += [bu[3], bd[3], cd[3], cu[3], b4, c4]
    where += [(-3, 0), (3, 0), (3, 1), (-3, 1), (4, 0), (4, 1)]
    pa1 = dot(dot_a_kernel, a_all[:N_A], vah, val)
    pb = dot(dot_b_kernel, b_all[:N_B], vbh, vbl)
    v_all = vah, val, vbh, vbl
    keep, give = last(at, where, a_all[N_A:] + b_all[N_B:], v_all, pa1, pb)

    partial = keep + send(give, OTHER_CORE)
    received = lax.all_to_all(
        partial, AXES, 0, 0, axis_index_groups=SAME_CORE, tiled=True
    )
    direct, messages = fold(received)
    mirror = lax.all_to_all(messages, AXES, 0, 0, axis_index_groups=SAME_COLUMN, tiled=True)

    vir_local = lax.dynamic_slice_in_dim(vir_energy, row * 4, 4, 0)
    occ_local = lax.dynamic_slice_in_dim(occ_energy, col, 1, 0)
    den = (
        vir_local[None, :, None] + vir_energy[None, None, :] - occ_local[:, None, None]
        - occ_energy[:, None, None]
    )
    out = finish(direct, mirror, rest.reshape(NJ, NAB), den.reshape(NJ, NAB))
    return out[None]


N_A, N_B = 13, 10


def solution(mesh):
    in_specs = (
        P("row", None, "col", None),
        P("row", None, "col", None),
        P("col", None, "row", None),
        P(),
        P(),
    )

    return jax.shard_map(
        on_device, mesh=mesh, in_specs=in_specs, out_specs=P("col", None, "row", None), check_vma=False
    )
```

```python
import jax
import jax.numpy as jnp
from jax import lax
from jax.experimental import pallas as pl
from jax.experimental.pallas import tpu as pltpu
from jax.sharding import PartitionSpec as P


NR, NC = 16, 16
NZ = 8
ND = 400
LANES = 128
NJ, NAB = 16, 256
TA, TB = 52, 27
F32, BF16 = jnp.float32, jnp.bfloat16
LAST_OUT = pltpu.VMEM

VMEM = pl.BlockSpec(memory_space=pltpu.VMEM)


def params(mib):
    return pltpu.CompilerParams(vmem_limit_bytes=mib << 20)


def on_chip(x):
    return pltpu.with_memory_space_constraint(x, pltpu.VMEM)


def rows_of_rest(x, n):
    parts = [x(c) for c in range(n)]
    if n < 8:
        parts.append(jnp.zeros(parts[0].shape[:-1] + (LANES - 16 * n,), F32))
    return jnp.concatenate(parts, axis=-1)


def pack_t_kernel(at_ref, t_ref, a_ref, b_ref):
    for ref, at, c0 in ((a_ref, 0, 0), (a_ref, 25, 8), (b_ref, 0, 16)):
        for c in range(8):
            for s in range(3):
                ref[at + 3 * c + s] = t_ref[c0 + c, :, LANES * s : LANES * (s + 1)]
        ref[at + 24] = rows_of_rest(lambda c: t_ref[c0 + c, :, 384:400], 8)
    a_ref[50] = t_ref[24, :, :LANES]
    a_ref[51] = t_ref[24, :, LANES : 2 * LANES]
    b_ref[25] = t_ref[24, :, 2 * LANES : 384]
    b_ref[26] = rows_of_rest(lambda c: t_ref[24, :, 384:400], 1)


def pack_t(at, t):
    return pl.pallas_call(
        pack_t_kernel,
        in_specs=[pl.BlockSpec(memory_space=pltpu.SMEM), VMEM],
        out_specs=(VMEM, VMEM),
        out_shape=(pltpu.VMEM((TA, NJ, LANES), F32), pltpu.VMEM((TB, NJ, LANES), F32)),
        compiler_params=params(4),
        name="pack_t",
    )(at, t)


def split(x):
    hi = x.astype(BF16)
    return hi, (x - hi.astype(F32)).astype(BF16)


def pack_v_group(v_ref, h_ref, l_ref):
    for c in range(8):
        for s in range(3):
            t = 3 * c + s
            h_ref[t], l_ref[t] = split(v_ref[c, :, LANES * s : LANES * (s + 1)])
    h_ref[24], l_ref[24] = split(rows_of_rest(lambda c: v_ref[c, :, 384:400], 8))


def rows_64(at):
    return pl.ds(pl.multiple_of(at * 64, 64), 64)


def pack_va_kernel(v_ref, w_ref, h_ref, l_ref):
    group, rows = pl.program_id(0), rows_64(pl.program_id(1))
    tiles = pl.ds(group * 25, 25)
    pack_v_group(v_ref, h_ref.at[tiles, rows], l_ref.at[tiles, rows])

    @pl.when(group == 1)
    def _():
        for s in range(2):
            tile = split(w_ref[0, :, LANES * s : LANES * (s + 1)])
            h_ref[50 + s, rows, :], l_ref[50 + s, rows, :] = tile


def pack_vb_kernel(v_ref, w_ref, h_ref, l_ref):
    rows = rows_64(pl.program_id(0))
    pack_v_group(v_ref, h_ref.at[:, rows], l_ref.at[:, rows])
    h_ref[25, rows, :], l_ref[25, rows, :] = split(w_ref[0, :, 2 * LANES : 384])
    h_ref[26, rows, :], l_ref[26, rows, :] = split(rows_of_rest(lambda c: w_ref[0, :, 384:400], 1))


def pack_va(v):
    out = pltpu.VMEM((TA, NAB, LANES), BF16)
    return pl.pallas_call(
        pack_va_kernel,
        grid=(2, 4),
        in_specs=[
            pl.BlockSpec((None, 8, 64, ND), lambda g, a: (a, g, 0, 0)),
            pl.BlockSpec((None, 1, 64, ND), lambda g, a: (a, 24, 0, 0)),
        ],
        out_specs=(VMEM, VMEM),
        out_shape=(out, out),
        compiler_params=params(8),
        name="pack_va",
    )(v, v)


def pack_vb(v):
    out = pltpu.VMEM((TB, NAB, LANES), BF16)
    return pl.pallas_call(
        pack_vb_kernel,
        grid=(4,),
        in_specs=[
            pl.BlockSpec((None, 8, 64, ND), lambda a: (a, 2, 0, 0)),
            pl.BlockSpec((None, 1, 64, ND), lambda a: (a, 24, 0, 0)),
        ],
        out_specs=(VMEM, VMEM),
        out_shape=(out, out),
        compiler_params=params(8),
        name="pack_vb",
    )(v, v)


def product(t_refs, vh_ref, vl_ref, first, n):
    cat = lambda ref: jnp.concatenate([ref[first + t] for t in range(n)], axis=-1)
    hi, lo = split(jnp.concatenate([cat(r) for r in t_refs], axis=0))
    vh, vl = cat(vh_ref), cat(vl_ref)
    dims = (((1,), (1,)), ((), ()))
    both = lax.dot_general(jnp.concatenate([hi, lo], axis=0), vh, dims, preferred_element_type=F32)
    m = hi.shape[0]
    return both[:m] + both[m:] + lax.dot_general(hi, vl, dims, preferred_element_type=F32)


def product_b(refs, vh, vl):
    total = product(refs, vh, vl, 0, 6)
    for first, n in ((6, 6), (12, 6), (18, 6), (24, 3)):
        total += product(refs, vh, vl, first, n)
    return total


def product_a(refs, vh, vl):
    step = lambda g: product(refs, vh, vl, g * 10, 10)
    total = lax.fori_loop(1, TA // 10, lambda g, total: total + step(g), step(0))
    return total + product(refs, vh, vl, 50, 2)


def dot_a_kernel(*refs):
    *t_refs, vh, vl, out = refs
    out[...] = product_a(t_refs, vh, vl)


def dot(kernel, blocks, vh, vl):
    args = [on_chip(x) for x in (*blocks, vh, vl)]
    return pl.pallas_call(
        kernel,
        in_specs=[VMEM] * len(args),
        out_specs=VMEM,
        out_shape=pltpu.VMEM((NJ * len(blocks), NAB), F32),
        compiler_params=params(8),
    )(*args)


def dot_b_kernel(*refs):
    *t_refs, vh, vl, out = refs
    out[...] = product_b(t_refs, vh, vl)


def absolute_row(row, dz, dy):
    return (((row >> 1) + dz) & (NZ - 1)) * 2 + ((row & 1) ^ dy)


def last_kernel(where, at_ref, *refs):
    *t_refs, vah, val, vbh, vbl, pa1, pb, keep, give, left, right = refs
    n_late = len(where) - pa1.shape[0] // NJ
    new_a = product_a(t_refs[:n_late], vah, val)
    new_b = product_b(t_refs[n_late:], vbh, vbl)
    row, core = at_ref[0], at_ref[1] & 1
    n_a, n_b = pa1.shape[0] // NJ, pb.shape[0] // NJ
    part = lambda x, q: x[NJ * q : NJ * (q + 1), :]
    for q, (dz, dy) in enumerate(where):
        block = part(pa1, q) if q < n_a else part(new_a, q - n_a)
        block += part(pb, q) if q < n_b else part(new_b, q - n_b)
        at = pl.ds(pl.multiple_of(absolute_row(row, dz, dy) * NJ, NJ), NJ)
        left[at, :] = block[:, :LANES]
        right[at, :] = block[:, LANES:]
    for other, out in enumerate((keep, give)):
        for m in range(NC // 2):
            k = 2 * m + (core ^ other)
            for ref, lanes in ((left, slice(0, LANES)), (right, slice(LANES, NAB))):
                out[(m - FIRST_CHIP) % 8, :NJ, lanes] = ref[pl.ds(pl.multiple_of(k * NJ, NJ), NJ), :]
                out[(m - FIRST_CHIP) % 8, NJ:, lanes] = ref[pl.ds(k, NJ, stride=NJ), :]


def last(at, where, blocks, v, pa1, pb):
    out = pltpu.VMEM((NC // 2, 2 * NJ, NAB), F32)
    args = [on_chip(x) for x in (*blocks, *v, pa1, pb)]
    return pl.pallas_call(
        lambda *refs: last_kernel(where, *refs),
        in_specs=[pl.BlockSpec(memory_space=pltpu.SMEM)] + [VMEM] * len(args),
        out_specs=(VMEM, VMEM),
        out_shape=(out, out),
        scratch_shapes=[pltpu.VMEM((NAB, LANES), F32)] * 2,
        compiler_params=params(8),
        name="last",
    )(at, *args)


def permute_lanes(x, source):
    lane = lax.broadcasted_iota(jnp.int32, (NAB, NAB), 1)
    one_hot = (lax.broadcasted_iota(jnp.int32, (NAB, NAB), 0) == source(lane)).astype(BF16)
    p1, r1 = x.astype(BF16), x - x.astype(BF16).astype(F32)
    p2 = r1.astype(BF16)
    p3 = (r1 - p2.astype(F32)).astype(BF16)
    y = jnp.dot(jnp.concatenate([p1, p2, p3], axis=0), one_hot, preferred_element_type=F32)
    m = x.shape[0]
    return y[:m] + y[m : 2 * m] + y[2 * m :]


def sum_rows(r_ref, rows):
    total = r_ref[0, rows, :]
    for k in range(1, NC // 2):
        total += r_ref[k, rows, :]
    return total


def fold_kernel(r_ref, e_ref):
    mixed = permute_lanes(
        sum_rows(r_ref, slice(NJ, 2 * NJ)),
        lambda n: ((n >> 2) & 3) * 64 + (n >> 4) * 4 + (n & 3),
    )
    zeros = jnp.zeros((8, LANES - 32), F32)
    for r in range(NR):
        lanes = slice(16 * r, 16 * (r + 1))
        e_ref[(r - FIRST_ROW) % NR] = jnp.concatenate([mixed[:8, lanes], mixed[8:, lanes], zeros], axis=-1)


def direct_kernel(r_ref, d_ref):
    d_ref[...] = sum_rows(r_ref, slice(0, NJ))


def from_received(kernel, r, out):
    return pl.pallas_call(
        kernel, in_specs=[VMEM], out_specs=VMEM, out_shape=out, compiler_params=params(4)
    )(on_chip(r))


def finish_kernel(d_ref, m_ref, rest_ref, den_ref, out_ref):
    halves = [
        jnp.concatenate([m_ref[(r - FIRST_ROW) % NR, :, 16 * h : 16 * (h + 1)] for r in range(NR)], axis=-1)
        for h in range(2)
    ]
    mirror = permute_lanes(
        jnp.concatenate(halves, axis=0), lambda n: ((n >> 2) & 15) * 16 + (n & 3) * 4 + (n >> 6)
    )
    value = (d_ref[...] + mirror + rest_ref[...]) / den_ref[...]
    for a in range(4):
        out_ref[:, a, :] = value[:, 64 * a : 64 * (a + 1)]


def finish(d, m, rest, den):
    args = [on_chip(x) for x in (d, m, rest, den)]
    return pl.pallas_call(
        finish_kernel,
        in_specs=[VMEM] * 4,
        out_specs=VMEM,
        out_shape=jax.ShapeDtypeStruct((NJ, 4, 64), F32),
        compiler_params=params(4),
        name="finish",
    )(*args)


AXES = ("row", "col")


def moves(dz=0, dy=0):
    pairs = []
    for z in range(NZ):
        for h in range(2):
            for k in range(NC):
                to = ((z + dz) % NZ * 2 + (h ^ dy)) * NC + k
                pairs.append(((z * 2 + h) * NC + k, to))
    return pairs


UP, DOWN, ACROSS = moves(dz=1), moves(dz=-1), moves(dy=1)
OTHER_CORE = [(i, i ^ 1) for i in range(NR * NC)]
FIRST_ROW = 9
SAME_COLUMN = [[(FIRST_ROW + m) % NR * NC + k for m in range(NR)] for k in range(NC)]
FIRST_CHIP = 5
SAME_CORE = [[r * NC + (FIRST_CHIP + m) % 8 * 2 + core for m in range(NC // 2)] for r in range(NR) for core in range(2)]


def send(x, where):
    return lax.ppermute(x, AXES, where)


def on_device(amplitudes, integrals, rest, occ_energy, vir_energy):
    row = lax.axis_index("row")
    col = lax.axis_index("col")
    at = jnp.stack([row, col])
    t = jnp.transpose(amplitudes, (0, 2, 1, 3))[0]
    a0, b0 = pack_t(at, pltpu.with_memory_space_constraint(t, pltpu.HBM))
    v = jnp.transpose(integrals, (0, 2, 1, 3))
    v = pltpu.with_memory_space_constraint(v, pltpu.HBM)
    vah, val = pack_va(v)
    vbh, vbl = pack_vb(v)

    au, ad, yu, yd = [a0], [a0], [send(a0, ACROSS)], [None]
    bx = send(b0, ACROSS)
    bu, bd, cu, cd = [b0], [b0], [bx], [bx]
    for _ in range(3):
        for chain, way in (
            (au, UP), (ad, DOWN), (bu, UP), (bd, DOWN),
            (cu, UP), (cd, DOWN),
        ):
            chain.append(send(chain[-1], way))
        yu.append(send(au[-1], ACROSS))
        yd.append(send(ad[-1], ACROSS))
    a4 = send(au[3], UP)
    a4x = send(yd[3], DOWN)
    b4 = send(bu[3], UP)
    c4 = send(cd[3], DOWN)

    a_all, b_all, where = [a0, yu[0]], [b0, bx], [(0, 0), (0, 1)]
    for s in (1, 2):
        a_all += [au[s], yu[s], ad[s], yd[s]]
        b_all += [bu[s], cu[s], bd[s], cd[s]]
        where += [(-s, 0), (-s, 1), (s, 0), (s, 1)]
    a_all += [au[3], ad[3], yd[3], yu[3], a4, a4x]
    b_all += [bu[3], bd[3], cd[3], cu[3], b4, c4]
    where += [(-3, 0), (3, 0), (3, 1), (-3, 1), (4, 0), (4, 1)]
    pa1 = dot(dot_a_kernel, a_all[:N_A], vah, val)
    pb = dot(dot_b_kernel, b_all[:N_B], vbh, vbl)
    v_all = vah, val, vbh, vbl
    keep, give = last(at, where, a_all[N_A:] + b_all[N_B:], v_all, pa1, pb)

    partial = keep + send(give, OTHER_CORE)
    received = lax.all_to_all(
        partial, AXES, 0, 0, axis_index_groups=SAME_CORE, tiled=True
    )
    messages = from_received(fold_kernel, received, LAST_OUT((NR, 8, LANES), F32))
    direct = from_received(direct_kernel, received, pltpu.VMEM((NJ, NAB), F32))
    mirror = lax.all_to_all(messages, AXES, 0, 0, axis_index_groups=SAME_COLUMN, tiled=True)

    vir_local = lax.dynamic_slice_in_dim(vir_energy, row * 4, 4, 0)
    occ_local = lax.dynamic_slice_in_dim(occ_energy, col, 1, 0)
    den = (
        vir_local[None, :, None] + vir_energy[None, None, :] - occ_local[:, None, None]
        - occ_energy[:, None, None]
    )
    out = finish(direct, mirror, rest.reshape(NJ, NAB), den.reshape(NJ, NAB))
    return out[None]


N_A, N_B = 13, 10


def solution(mesh):
    in_specs = (
        P("row", None, "col", None),
        P("row", None, "col", None),
        P("col", None, "row", None),
        P(),
        P(),
    )

    return jax.shard_map(
        on_device, mesh=mesh, in_specs=in_specs, out_specs=P("col", None, "row", None), check_vma=False
    )
```
